32 devices in a mesh: dp: 8 (over z, x), seq: 4 (over y, core).
Axes of the slice: x: 2, y: 2, z: 4, core: 2. Of those that a mesh axis runs over, the one named last changes fastest.
Arguments:
- tokens: bfloat16 [16, 1024, 1600], P('dp', 'seq'), may hold values from -6 to 6
- span_order: int32 [16, 8], P('dp'), may hold values from 0 to 7, each once within a row
- qkv_weight: bfloat16 [1600, 4800], P('seq', 'dp'), may hold values from -0.15625 to 0.15625
- out_weight: bfloat16 [1600, 1600], P('seq', 'dp'), may hold values from -0.625 to 0.625
- fc_weight: bfloat16 [1600, 6400], P('seq', 'dp'), may hold values from -0.15625 to 0.15625
- proj_weight: bfloat16 [6400, 1600], P('seq', 'dp'), may hold values from -0.078125 to 0.078125
- ln1_gain: bfloat16 [1600], P('seq'), may hold values from 0.5 to 1.5
- ln1_bias: bfloat16 [1600], P('seq'), may hold values from -1.75 to 1.75
- qv_bias: bfloat16 [2, 1600], P(None, 'seq'), may hold values from -1.75 to 1.75
- out_bias: bfloat16 [1600], P('seq'), may hold values from -1.75 to 1.75
- ln2_gain: bfloat16 [1600], P('seq'), may hold values from 0.5 to 1.5
- ln2_bias: bfloat16 [1600], P('seq'), may hold values from -1.75 to 1.75
- fc_bias: bfloat16 [6400], P('seq'), may hold values from -1.75 to 1.75
- proj_bias: bfloat16 [1600], P('seq'), may hold values from -1.75 to 1.75
- out_grad: bfloat16 [16, 1024, 1600], P('dp', 'seq'), may hold values from -6 to 6
Outputs:
- output: bfloat16 [16, 1024, 1600], P('dp', 'seq')
- input_grad: bfloat16 [16, 1024, 1600], P('dp', 'seq')
- qkv_weight_grad: float32 [1600, 4800], P('seq', 'dp')
- out_weight_grad: float32 [1600, 1600], P('seq', 'dp')
- fc_weight_grad: float32 [1600, 6400], P('seq', 'dp')
- proj_weight_grad: float32 [6400, 1600], P('seq', 'dp')
- ln1_gain_grad: float32 [1600], P('seq')
- ln1_bias_grad: float32 [1600], P('seq')
- qv_bias_grad: float32 [2, 1600], P(None, 'seq')
- out_bias_grad: float32 [1600], P('seq')
- ln2_gain_grad: float32 [1600], P('seq')
- ln2_bias_grad: float32 [1600], P('seq')
- fc_bias_grad: float32 [6400], P('seq')
- proj_bias_grad: float32 [1600], P('seq')
The draws below stay inside these ranges and needn't reach their ends.
Inputs may be any that keep to these rules, and one draw needn't show every extreme that they name: `span_order`: each row is a permutation of the spans 0 to 7 of its sequence.
All inputs are finite; a program needn't handle non-finite values.
Results may differ from the reference program's by a relative error of at most 0.02.
Values may be sent and summed in bfloat16 or wider, within the bound.
A program may use at most 384 MiB of HBM per device.

```python
import jax
import jax.numpy as jnp
from jax import lax

D = 1600
HEADS = 25
HEAD = 64
FF = 6400
LEN = 1024
SEQS = 16
SPANS = 8
SPAN = 128


def shard_levels(key, dims, cuts, least, largest):
    factor_of, own = 1.0, jax.random.fold_in(key, 6)
    for axis_at, blocks in cuts:
        steps = jnp.exp(jax.random.uniform(jax.random.fold_in(own, axis_at), (blocks,), jnp.float32, least / len(cuts), largest / len(cuts)))
        factor_of = factor_of * jnp.repeat(steps, dims[axis_at] // blocks).reshape([-1 if axis == axis_at else 1 for axis in range(len(dims))])
    return factor_of


def gaussian(rng, extent, scale, limit, cuts=(), kind=jnp.bfloat16):
    drawn = jax.random.normal(rng, extent, jnp.float32) * scale
    if len(cuts) > 0:
        drawn = shard_levels(rng, extent, cuts, -0.22, 0.18) * drawn
    return jnp.clip(drawn, min=-limit, max=limit).astype(kind)


def setup_inputs(seed: int = 0) -> dict:
    key_of = jax.random.split(jax.random.key(seed), 16)
    tokens = gaussian(key_of[0], (SEQS, LEN, D), 1.0, 6.0, ((0, 8), (1, 4)))
    span_order = jax.vmap(lambda own: jax.random.permutation(own, SPANS))(jax.random.split(key_of[1], SEQS)).reshape((SEQS, SPANS)).astype(jnp.int32)
    qkv_weight = gaussian(key_of[2], (D, 3 * D), D ** -0.5, 0.15625, ((0, 4), (1, 8)))
    out_weight = gaussian(key_of[3], (D, D), (D // 16) ** -0.5, 0.625, ((0, 4), (1, 8)))
    fc_weight = gaussian(key_of[4], (D, FF), D ** -0.5, 0.15625, ((0, 4), (1, 8)))
    proj_weight = gaussian(key_of[5], (FF, D), FF ** -0.5, 0.078125, ((0, 4), (1, 8)))
    ln1_gain = jnp.clip(1.0 + 0.1 * jax.random.normal(key_of[6], (D,), jnp.float32), 0.5, 1.5).astype(jnp.bfloat16)
    ln1_bias = gaussian(key_of[7], (D,), 0.3, 1.75, ((0, 4),))
    qv_bias = gaussian(key_of[8], (2, D), 0.3, 1.75, ((1, 4),))
    out_bias = gaussian(key_of[9], (D,), 0.3, 1.75, ((0, 4),))
    ln2_gain = jnp.clip(1.0 + 0.1 * jax.random.normal(key_of[10], (D,), jnp.float32), 0.5, 1.5).astype(jnp.bfloat16)
    ln2_bias = gaussian(key_of[11], (D,), 0.3, 1.75, ((0, 4),))
    fc_bias = gaussian(key_of[12], (FF,), 0.3, 1.75, ((0, 4),))
    proj_bias = gaussian(key_of[13], (D,), 0.3, 1.75, ((0, 4),))
    out_grad = gaussian(key_of[14], (SEQS, LEN, D), 1.0, 6.0, ((0, 8), (1, 4)))
    return dict(tokens=tokens, span_order=span_order, qkv_weight=qkv_weight, out_weight=out_weight, fc_weight=fc_weight, proj_weight=proj_weight, ln1_gain=ln1_gain, ln1_bias=ln1_bias, qv_bias=qv_bias, out_bias=out_bias, ln2_gain=ln2_gain, ln2_bias=ln2_bias, fc_bias=fc_bias, proj_bias=proj_bias, out_grad=out_grad)


@jax.custom_vjp
def low(v):
    return lax.optimization_barrier(v.astype(jnp.bfloat16)).astype(jnp.float32)

@jax.custom_vjp
def low_back(v):
    return v

def low_keep(v):
    return (low(v), None)

def low_pass(kept, grad):
    return (grad,)

def back_keep(v):
    return (v, None)

def back_low(kept, grad):
    return (low(grad),)
low.defvjp(low_keep, low_pass)
low_back.defvjp(back_keep, back_low)
HIGHEST_PRECISION = lax.Precision.HIGHEST

def layer_norm(value, gain, shift):
    center = lax.optimization_barrier(jnp.mean(value, axis=-1, keepdims=True))
    offsets = value - center
    spread = lax.optimization_barrier(jnp.mean(offsets * offsets, axis=-1, keepdims=True))
    return offsets * lax.rsqrt(spread + 1e-05) * gain + shift

def product(left, right):
    return jnp.dot(left, right, precision=HIGHEST_PRECISION, preferred_element_type=jnp.float32)

def one_sequence(params, tokens, order):
    qkv_weight, out_weight, fc_weight, proj_weight, ln1_gain, ln1_bias, qv_bias, out_bias, ln2_gain, ln2_bias, fc_bias, proj_bias = params
    rows = jnp.arange(LEN, dtype=jnp.int32)
    places = order[rows // SPAN] * SPAN + rows % SPAN
    normed_one = low(layer_norm(tokens, ln1_gain, ln1_bias))
    packed_shift = jnp.concatenate([qv_bias[0], jnp.zeros((D,), jnp.float32), qv_bias[1]])
    packed = low_back(low(product(normed_one, qkv_weight) + packed_shift))
    split = packed.reshape(LEN, 3, HEADS, HEAD)
    scores = jnp.einsum('qhd,khd->hqk', split[:, 0], split[:, 1], precision=HIGHEST_PRECISION) * HEAD ** (-0.5)
    scores = low_back(scores)
    allowed = places[None, :] <= places[:, None]
    scores = jnp.where(allowed[None], scores, -1e+30)
    row_max = lax.optimization_barrier(jnp.max(scores, axis=-1, keepdims=True))
    weights = jnp.exp(scores - row_max)
    probs = low(weights / lax.optimization_barrier(jnp.sum(weights, axis=-1, keepdims=True)))
    attended = jnp.einsum('hqk,khd->qhd', probs, split[:, 2], precision=HIGHEST_PRECISION).reshape(LEN, D)
    attended = low_back(low(attended))
    middle = tokens + low_back(product(attended, out_weight) + out_bias)
    normed_two = low(layer_norm(middle, ln2_gain, ln2_bias))
    hidden_pre = low_back(product(normed_two, fc_weight) + fc_bias)
    hidden = low(jax.nn.gelu(hidden_pre, approximate=True))
    return middle + (product(hidden, proj_weight) + proj_bias)

def reference(tokens, span_order, qkv_weight, out_weight, fc_weight, proj_weight, ln1_gain, ln1_bias, qv_bias, out_bias, ln2_gain, ln2_bias, fc_bias, proj_bias, out_grad):
    params = tuple((item.astype(jnp.float32) for item in (qkv_weight, out_weight, fc_weight, proj_weight, ln1_gain, ln1_bias, qv_bias, out_bias, ln2_gain, ln2_bias, fc_bias, proj_bias)))
    inputs = tokens.astype(jnp.float32)
    checked = jax.checkpoint(one_sequence)

    def forward(weights, values):

        def scan_step(carry, item):
            return (carry, checked(weights, item[0], item[1]))
        return lax.scan(scan_step, jnp.float32(0.0), (values, span_order))[1]
    result, pullback = jax.vjp(forward, params, inputs)
    param_grads, input_grads = pullback(out_grad.astype(jnp.float32))
    return (result.astype(jnp.bfloat16), input_grads.astype(jnp.bfloat16), param_grads[0], param_grads[1], param_grads[2], param_grads[3], param_grads[4], param_grads[5], param_grads[6], param_grads[7], param_grads[8], param_grads[9], param_grads[10], param_grads[11])
```

```python
import functools

import jax
import jax.numpy as jnp
from jax import lax
from jax.experimental import pallas as pl
from jax.experimental.pallas import tpu as pltpu
from jax.sharding import PartitionSpec as P

HEAD = 64
MB_SEQS = 1


def layer_norm(value, gain, shift):
    center = jnp.mean(value, axis=-1, keepdims=True)
    offsets = value - center
    spread = jnp.mean(offsets * offsets, axis=-1, keepdims=True)
    return offsets * lax.rsqrt(spread + 1e-05) * gain + shift


def norm_grad(value, gain, shift, cotangent):
    result, pullback = jax.vjp(layer_norm, value, gain, shift)
    return pullback(cotangent)


def smooth_gate(value):
    return jax.nn.gelu(value, approximate=True)


def gate_grad(value, cotangent):
    result, pullback = jax.vjp(smooth_gate, value)
    return pullback(cotangent)[0]


def place_table(order, length, block):
    rows = jnp.arange(length, dtype=jnp.int32)
    span_ids = jnp.arange(order.shape[-1], dtype=jnp.int32)
    picks = (rows // block)[:, None] == span_ids[None, :]
    starts = jnp.sum(jnp.where(picks[None], order[:, None, :], 0), axis=-1)
    return starts * block + rows % block


def spread_product(left, columns):
    return jnp.dot(
        left, lax.all_gather(columns, "dp", axis=1, tiled=True), preferred_element_type=jnp.float32
    )


def back_product(grads, columns):
    return lax.dot_general(
        grads,
        lax.all_gather(columns, "dp", axis=1, tiled=True),
        (((1,), (1,)), ((), ())),
        preferred_element_type=jnp.float32,
    )


def masked_scores(queries, key_heads, query_places, key_places):
    scale = queries.shape[-1] ** (-0.5)
    scores = (
        jnp.einsum("qhd,khd->hqk", queries, key_heads, preferred_element_type=jnp.float32) * scale
    )
    allowed = key_places[None, :] <= query_places[:, None]
    return (jnp.where(allowed[None], scores, -1e30), allowed)


def attend(item):
    queries, key_rows, value_rows, query_places, key_places = item
    heads = queries.shape[1]
    key_heads = key_rows.reshape(key_rows.shape[0], heads, -1)
    value_heads = value_rows.reshape(value_rows.shape[0], heads, -1)
    scores, allowed = masked_scores(queries, key_heads, query_places, key_places)
    row_max = jnp.max(scores, axis=-1, keepdims=True)
    weights = jnp.exp(scores - row_max)
    row_total = jnp.sum(weights, axis=-1, keepdims=True)
    probs = (weights / row_total).astype(jnp.bfloat16)
    attended = jnp.einsum("hqk,khd->qhd", probs, value_heads, preferred_element_type=jnp.float32)
    return (attended, (row_max + jnp.log(row_total))[:, :, 0])


def attend_back(item):
    queries, key_rows, value_rows, query_places, key_places, log_total, grad_out = item
    heads = queries.shape[1]
    scale = queries.shape[-1] ** (-0.5)
    key_heads = key_rows.reshape(key_rows.shape[0], heads, -1)
    value_heads = value_rows.reshape(value_rows.shape[0], heads, -1)
    scores, allowed = masked_scores(queries, key_heads, query_places, key_places)
    probs = jnp.where(allowed[None], jnp.exp(scores - log_total[:, :, None]), 0.0)
    grad_probs = jnp.einsum(
        "qhd,khd->hqk", grad_out, value_heads, preferred_element_type=jnp.float32
    )
    centre = jnp.sum(probs * grad_probs, axis=-1, keepdims=True)
    grad_scores = (probs * (grad_probs - centre)).astype(jnp.bfloat16)
    grad_queries = (
        jnp.einsum("hqk,khd->qhd", grad_scores, key_heads, preferred_element_type=jnp.float32)
        * scale
    )
    grad_keys = (
        jnp.einsum("hqk,qhd->khd", grad_scores, queries, preferred_element_type=jnp.float32) * scale
    )
    grad_values = jnp.einsum(
        "hqk,qhd->khd", probs.astype(jnp.bfloat16), grad_out, preferred_element_type=jnp.float32
    )
    query_count = queries.shape[0]
    key_count = key_rows.shape[0]
    return (
        grad_queries.reshape(query_count, -1),
        grad_keys.reshape(key_count, -1),
        grad_values.reshape(key_count, -1),
    )


def local(
    tokens,
    span_order,
    qkv_weight,
    out_weight,
    fc_weight,
    proj_weight,
    ln1_gain,
    ln1_bias,
    qv_bias,
    out_bias,
    ln2_gain,
    ln2_bias,
    fc_bias,
    proj_bias,
    out_grad,
):
    seq_count = lax.axis_size("seq")
    dp_count = lax.axis_size("dp")
    local_len = tokens.shape[1]
    width = tokens.shape[2]
    full_len = local_len * seq_count
    block = full_len // span_order.shape[1]
    group = MB_SEQS
    rounds = tokens.shape[0] // group
    row_count = group * local_len
    heads = width // HEAD
    hidden_width = fc_weight.shape[1] * dp_count
    places = place_table(span_order, full_len, block)
    own_places = lax.dynamic_slice_in_dim(places, lax.axis_index("seq") * local_len, local_len, 1)
    local_weights = (qkv_weight, out_weight, fc_weight, proj_weight)
    weight_sums = [
        jnp.zeros((item.shape[0] * seq_count, item.shape[1] * dp_count), jnp.float32)
        for item in local_weights
    ]
    vector_shapes = (
        (width,),
        (width,),
        (2, width),
        (width,),
        (width,),
        (width,),
        (hidden_width,),
        (width,),
    )
    vector_sums = [jnp.zeros(shape, jnp.float32) for shape in vector_shapes]
    outputs = []
    input_grads = []
    for index in range(rounds):
        first = index * group
        batch_tokens = tokens[first : first + group]
        batch_grad = out_grad[first : first + group]
        batch_places = places[first : first + group]
        batch_own = own_places[first : first + group]
        gathered = (
            lax.all_gather(qkv_weight, "seq", axis=0, tiled=True),
            lax.all_gather(out_weight, "seq", axis=0, tiled=True),
            lax.all_gather(fc_weight, "seq", axis=0, tiled=True),
            lax.all_gather(proj_weight, "seq", axis=0, tiled=True),
            lax.all_gather(ln1_gain, "seq", axis=0, tiled=True),
            lax.all_gather(ln1_bias, "seq", axis=0, tiled=True),
            lax.all_gather(qv_bias, "seq", axis=1, tiled=True),
            lax.all_gather(out_bias, "seq", axis=0, tiled=True),
            lax.all_gather(ln2_gain, "seq", axis=0, tiled=True),
            lax.all_gather(ln2_bias, "seq", axis=0, tiled=True),
            lax.all_gather(fc_bias, "seq", axis=0, tiled=True),
            lax.all_gather(proj_bias, "seq", axis=0, tiled=True),
        )
        gain_one = gathered[4].astype(jnp.float32)
        shift_one = gathered[5].astype(jnp.float32)
        qv_full = gathered[6].astype(jnp.float32)
        out_shift = gathered[7].astype(jnp.float32)
        gain_two = gathered[8].astype(jnp.float32)
        shift_two = gathered[9].astype(jnp.float32)
        fc_shift = gathered[10].astype(jnp.float32)
        proj_shift = gathered[11].astype(jnp.float32)
        tokens_in = batch_tokens.reshape(row_count, width).astype(jnp.float32)
        normed_one = layer_norm(tokens_in, gain_one, shift_one).astype(jnp.bfloat16)
        packed_shift = jnp.concatenate([qv_full[0], jnp.zeros((width,), jnp.float32), qv_full[1]])
        packed = (spread_product(normed_one, gathered[0]) + packed_shift).astype(jnp.bfloat16)
        queries = packed[:, :width].reshape(group, local_len, heads, HEAD)
        key_local = packed[:, width : 2 * width].reshape(group, local_len, width)
        value_local = packed[:, 2 * width :].reshape(group, local_len, width)
        key_rows, value_rows = (
            lax.all_gather(key_local, "seq", axis=1, tiled=True),
            lax.all_gather(value_local, "seq", axis=1, tiled=True),
        )
        attended, log_total = lax.map(
            attend, (queries, key_rows, value_rows, batch_own, batch_places)
        )
        attended_low = attended.reshape(row_count, width).astype(jnp.bfloat16)
        middle = tokens_in + (spread_product(attended_low, gathered[1]) + out_shift)
        normed_two = layer_norm(middle, gain_two, shift_two).astype(jnp.bfloat16)
        hidden_pre = spread_product(normed_two, gathered[2]) + fc_shift
        hidden_low = smooth_gate(hidden_pre).astype(jnp.bfloat16)
        result = middle + (spread_product(hidden_low, gathered[3]) + proj_shift)
        outputs.append(result.astype(jnp.bfloat16).reshape(group, local_len, width))
        columns = (
            lax.all_gather(qkv_weight, "seq", axis=0, tiled=True),
            lax.all_gather(out_weight, "seq", axis=0, tiled=True),
            lax.all_gather(fc_weight, "seq", axis=0, tiled=True),
            lax.all_gather(proj_weight, "seq", axis=0, tiled=True),
        )
        grad_rows = batch_grad.reshape(row_count, width)
        grad_hidden = back_product(grad_rows, columns[3])
        grad_pre = gate_grad(hidden_pre, grad_hidden).astype(jnp.bfloat16)
        grad_normed_two = back_product(grad_pre, columns[2])
        grad_mid_norm, grad_gain_two, grad_shift_two = norm_grad(
            middle, gain_two, shift_two, grad_normed_two
        )
        grad_middle = grad_rows.astype(jnp.float32) + grad_mid_norm
        grad_branch = grad_middle.astype(jnp.bfloat16)
        grad_attended = back_product(grad_branch, columns[1]).astype(jnp.bfloat16)
        grad_attended = grad_attended.reshape(group, local_len, heads, HEAD)
        key_back, value_back = (
            lax.all_gather(key_local, "seq", axis=1, tiled=True),
            lax.all_gather(value_local, "seq", axis=1, tiled=True),
        )
        grad_queries, grad_keys, grad_values = lax.map(
            attend_back,
            (queries, key_back, value_back, batch_own, batch_places, log_total, grad_attended),
        )
        grad_keys, grad_values = (
            lax.psum_scatter(
                grad_keys.astype(jnp.bfloat16), "seq", scatter_dimension=1, tiled=True
            ).astype(jnp.float32),
            lax.psum_scatter(
                grad_values.astype(jnp.bfloat16), "seq", scatter_dimension=1, tiled=True
            ).astype(jnp.float32),
        )
        grad_packed = jnp.concatenate([grad_queries, grad_keys, grad_values], axis=-1)
        grad_packed = grad_packed.reshape(row_count, 3 * width).astype(jnp.bfloat16)
        grad_normed_one = back_product(grad_packed, columns[0])
        grad_in_norm, grad_gain_one, grad_shift_one = norm_grad(
            tokens_in, gain_one, shift_one, grad_normed_one
        )
        input_grads.append(
            (grad_middle + grad_in_norm).astype(jnp.bfloat16).reshape(group, local_len, width)
        )
        pairs = (
            (normed_one, grad_packed),
            (attended_low, grad_branch),
            (normed_two, grad_pre),
            (hidden_low, grad_rows),
        )
        for slot in range(4):
            left, right = pairs[slot]
            weight_sums[slot] = weight_sums[slot] + lax.dot_general(
                left, right, (((0,), (0,)), ((), ())), preferred_element_type=jnp.float32
            )
        qv_grad = jnp.stack(
            [
                jnp.sum(grad_packed[:, :width], axis=0, dtype=jnp.float32),
                jnp.sum(grad_packed[:, 2 * width :], axis=0, dtype=jnp.float32),
            ]
        )
        vector_terms = (
            grad_gain_one,
            grad_shift_one,
            qv_grad,
            jnp.sum(grad_branch, axis=0, dtype=jnp.float32),
            grad_gain_two,
            grad_shift_two,
            jnp.sum(grad_pre, axis=0, dtype=jnp.float32),
            jnp.sum(grad_rows, axis=0, dtype=jnp.float32),
        )
        vector_sums = [vector_sums[slot] + vector_terms[slot] for slot in range(8)]
    weight_parts = (
        lax.psum_scatter(
            weight_sums[0].astype(jnp.bfloat16), "dp", scatter_dimension=1, tiled=True
        ).astype(jnp.float32),
        lax.psum_scatter(
            weight_sums[1].astype(jnp.bfloat16), "dp", scatter_dimension=1, tiled=True
        ).astype(jnp.float32),
        lax.psum_scatter(
            weight_sums[2].astype(jnp.bfloat16), "dp", scatter_dimension=1, tiled=True
        ).astype(jnp.float32),
        lax.psum_scatter(
            weight_sums[3].astype(jnp.bfloat16), "dp", scatter_dimension=1, tiled=True
        ).astype(jnp.float32),
    )
    vector_parts = (
        lax.psum(vector_sums[0].astype(jnp.bfloat16), "dp").astype(jnp.float32),
        lax.psum(vector_sums[1].astype(jnp.bfloat16), "dp").astype(jnp.float32),
        lax.psum(vector_sums[2].astype(jnp.bfloat16), "dp").astype(jnp.float32),
        lax.psum(vector_sums[3].astype(jnp.bfloat16), "dp").astype(jnp.float32),
        lax.psum(vector_sums[4].astype(jnp.bfloat16), "dp").astype(jnp.float32),
        lax.psum(vector_sums[5].astype(jnp.bfloat16), "dp").astype(jnp.float32),
        lax.psum(vector_sums[6].astype(jnp.bfloat16), "dp").astype(jnp.float32),
        lax.psum(vector_sums[7].astype(jnp.bfloat16), "dp").astype(jnp.float32),
    )
    finals = (
        lax.psum_scatter(
            weight_parts[0].astype(jnp.bfloat16), "seq", scatter_dimension=0, tiled=True
        ).astype(jnp.float32),
        lax.psum_scatter(
            weight_parts[1].astype(jnp.bfloat16), "seq", scatter_dimension=0, tiled=True
        ).astype(jnp.float32),
        lax.psum_scatter(
            weight_parts[2].astype(jnp.bfloat16), "seq", scatter_dimension=0, tiled=True
        ).astype(jnp.float32),
        lax.psum_scatter(
            weight_parts[3].astype(jnp.bfloat16), "seq", scatter_dimension=0, tiled=True
        ).astype(jnp.float32),
        lax.psum_scatter(
            vector_parts[0].astype(jnp.bfloat16), "seq", scatter_dimension=0, tiled=True
        ).astype(jnp.float32),
        lax.psum_scatter(
            vector_parts[1].astype(jnp.bfloat16), "seq", scatter_dimension=0, tiled=True
        ).astype(jnp.float32),
        lax.psum_scatter(
            vector_parts[2].astype(jnp.bfloat16), "seq", scatter_dimension=1, tiled=True
        ).astype(jnp.float32),
        lax.psum_scatter(
            vector_parts[3].astype(jnp.bfloat16), "seq", scatter_dimension=0, tiled=True
        ).astype(jnp.float32),
        lax.psum_scatter(
            vector_parts[4].astype(jnp.bfloat16), "seq", scatter_dimension=0, tiled=True
        ).astype(jnp.float32),
        lax.psum_scatter(
            vector_parts[5].astype(jnp.bfloat16), "seq", scatter_dimension=0, tiled=True
        ).astype(jnp.float32),
        lax.psum_scatter(
            vector_parts[6].astype(jnp.bfloat16), "seq", scatter_dimension=0, tiled=True
        ).astype(jnp.float32),
        lax.psum_scatter(
            vector_parts[7].astype(jnp.bfloat16), "seq", scatter_dimension=0, tiled=True
        ).astype(jnp.float32),
    )
    return (
        jnp.concatenate(outputs, axis=0),
        jnp.concatenate(input_grads, axis=0),
        finals[0],
        finals[1],
        finals[2],
        finals[3],
        finals[4],
        finals[5],
        finals[6],
        finals[7],
        finals[8],
        finals[9],
        finals[10],
        finals[11],
    )


BF = jnp.bfloat16
F32 = jnp.float32
PAIR = 2 * HEAD
NEG = -1e30


def mm(left, right, contract):
    return lax.dot_general(left, right, (contract, ((), ())), preferred_element_type=F32)


def nn(left, right):
    return mm(left, right, ((1,), (0,)))


def nt(left, right):
    return mm(left, right, ((1,), (1,)))


def tn(left, right):
    return mm(left, right, ((0,), (0,)))


def sort_rows(pos_ref, src, dst, chunk, count):
    for j in range(count):
        dst[pl.ds(j * chunk, chunk), :] = src[
            pl.ds(pl.multiple_of(pos_ref[j] * chunk, chunk), chunk), :
        ]


def take_rows(pos_ref, src, first, chunk, count):
    parts = [
        src[pl.ds(pl.multiple_of(pos_ref[first + j] * chunk, chunk), chunk), :]
        for j in range(count)
    ]
    return jnp.concatenate(parts, axis=0)


def put_rows(pos_ref, dst, first, chunk, count, value):
    for j in range(count):
        dst[pl.ds(pl.multiple_of(pos_ref[first + j] * chunk, chunk), chunk), :] = value[
            j * chunk : (j + 1) * chunk
        ]


def head_lanes(value, head):
    lane = lax.broadcasted_iota(jnp.int32, value.shape, 1)
    inside = (lane < HEAD) if head == 0 else (lane >= HEAD)
    return jnp.where(inside, value, jnp.zeros_like(value))


def causal(block):
    key = lax.broadcasted_iota(jnp.int32, block.shape, 0)
    query = lax.broadcasted_iota(jnp.int32, block.shape, 1)
    return key <= query


def attend_kernel(
    chunk, count, step, pos_ref, keep_ref, q_ref, k_ref, v_ref, o_ref, lse_ref, ks, vt
):
    pair = pl.program_id(0)
    sort_rows(pos_ref, k_ref, ks, chunk, count)
    for j in range(count):
        rows = v_ref[pl.ds(pl.multiple_of(pos_ref[j] * chunk, chunk), chunk), :]
        vt[:, pl.ds(j * chunk, chunk)] = rows.T
    tile = step * chunk
    for block in range(count // step):
        q_rows = take_rows(pos_ref, q_ref, block * step, chunk, step) * HEAD ** (-0.5)
        start = block * tile
        done = []
        for head in range(2):
            q_head = head_lanes(q_rows.astype(BF), head)
            diag = nt(ks[pl.ds(start, tile), :], q_head)
            diag = jnp.where(causal(diag), diag, NEG)
            top = jnp.max(diag, axis=0, keepdims=True)
            if block > 0:
                full = nt(ks[pl.ds(0, start), :], q_head)
                top = jnp.maximum(top, jnp.max(full, axis=0, keepdims=True))
            p_diag = jnp.exp(diag - top)
            total = jnp.sum(p_diag, axis=0, keepdims=True)
            out = nn(vt[:, pl.ds(start, tile)], p_diag.astype(BF))
            if block > 0:
                p_full = jnp.exp(full - top)
                total = total + jnp.sum(p_full, axis=0, keepdims=True)
                out = out + nn(vt[:, pl.ds(0, start)], p_full.astype(BF))
            lse_ref[pl.ds(head, 1), pl.ds(start, tile)] = top + jnp.log(total)
            out = out / total
            done.append(jnp.where(keep_ref[2 * pair + head] > 0, out, jnp.zeros_like(out)))
        merged = jnp.concatenate([done[0][:HEAD], done[1][HEAD:]], axis=0)
        put_rows(pos_ref, o_ref, block * step, chunk, step, merged.T.astype(BF))


def attend_back_kernel(
    chunk,
    count,
    step,
    pos_ref,
    keep_ref,
    q_ref,
    k_ref,
    v_ref,
    do_ref,
    lse_ref,
    dq_ref,
    dk_ref,
    dv_ref,
    ks,
    vs,
    kt,
    dks,
    dvs,
):
    pair = pl.program_id(0)
    sort_rows(pos_ref, k_ref, ks, chunk, count)
    sort_rows(pos_ref, v_ref, vs, chunk, count)
    for j in range(count):
        kt[:, pl.ds(j * chunk, chunk)] = ks[pl.ds(j * chunk, chunk), :].T
    tile = step * chunk
    for block in range(count // step):
        q_rows = (take_rows(pos_ref, q_ref, block * step, chunk, step) * HEAD ** (-0.5)).astype(BF)
        do_rows = take_rows(pos_ref, do_ref, block * step, chunk, step)
        start = block * tile
        dq = []
        for head in range(2):
            q_head = head_lanes(q_rows, head)
            do_head = head_lanes(do_rows, head)
            do_head = jnp.where(keep_ref[2 * pair + head] > 0, do_head, jnp.zeros_like(do_head))
            lse = lse_ref[pl.ds(head, 1), pl.ds(start, tile)]
            spans = [(start, tile)] if block == 0 else [(0, start), (start, tile)]
            probs = []
            grads = []
            delta = jnp.zeros_like(lse)
            for first, size in spans:
                s = nt(ks[pl.ds(first, size), :], q_head)
                p = jnp.exp(s - lse)
                if first == start:
                    p = jnp.where(causal(p), p, jnp.zeros_like(p))
                g = nt(vs[pl.ds(first, size), :], do_head)
                delta = delta + jnp.sum(p * g, axis=0, keepdims=True)
                probs.append(p)
                grads.append(g)
            dq_head = jnp.zeros((PAIR, tile), F32)
            for (first, size), p, g in zip(spans, probs, grads):
                ds = (p * (g - delta)).astype(BF)
                dq_head = dq_head + nn(kt[:, pl.ds(first, size)], ds)
                dk = nn(ds, q_head)
                dv = nn(p.astype(BF), do_head)
                if first == start and head == 0:
                    dks[pl.ds(first, size), :] = dk
                    dvs[pl.ds(first, size), :] = dv
                else:
                    dks[pl.ds(first, size), :] += dk
                    dvs[pl.ds(first, size), :] += dv
            dq.append(dq_head)
        merged = jnp.concatenate([dq[0][:HEAD], dq[1][HEAD:]], axis=0) * HEAD ** (-0.5)
        put_rows(pos_ref, dq_ref, block * step, chunk, step, merged.T.astype(BF))
    put_rows(pos_ref, dk_ref, 0, chunk, count, dks[...].astype(BF))
    put_rows(pos_ref, dv_ref, 0, chunk, count, dvs[...].astype(BF))


def attend_fast(pos, keep, queries, keys, values):
    length, wide = queries.shape
    count = pos.shape[0]
    chunk = length // count
    pairs = wide // PAIR
    tile = pl.BlockSpec((length, PAIR), lambda p, *_: (0, p))
    return pl.pallas_call(
        functools.partial(attend_kernel, chunk, count, 2),
        out_shape=(
            jax.ShapeDtypeStruct((length, wide), BF),
            jax.ShapeDtypeStruct((pairs * 8, length), F32),
        ),
        grid_spec=pltpu.PrefetchScalarGridSpec(
            num_scalar_prefetch=2,
            grid=(pairs,),
            in_specs=[tile, tile, tile],
            out_specs=[tile, pl.BlockSpec((8, length), lambda p, *_: (p, 0))],
            scratch_shapes=[pltpu.VMEM((length, PAIR), BF), pltpu.VMEM((PAIR, length), BF)],
        ),
        cost_estimate=pl.CostEstimate(
            flops=4 * length * length * wide,
            transcendentals=length * length * wide // PAIR,
            bytes_accessed=8 * length * wide,
        ),
        name="attend",
    )(pos, keep, queries, keys, values)


def attend_back_fast(pos, keep, queries, keys, values, grad_out, lse):
    length, wide = queries.shape
    count = pos.shape[0]
    chunk = length // count
    pairs = wide // PAIR
    tile = pl.BlockSpec((length, PAIR), lambda p, *_: (0, p))
    return pl.pallas_call(
        functools.partial(attend_back_kernel, chunk, count, 2),
        out_shape=(jax.ShapeDtypeStruct((length, wide), BF),) * 3,
        grid_spec=pltpu.PrefetchScalarGridSpec(
            num_scalar_prefetch=2,
            grid=(pairs,),
            in_specs=[tile, tile, tile, tile, pl.BlockSpec((8, length), lambda p, *_: (p, 0))],
            out_specs=[tile, tile, tile],
            scratch_shapes=[
                pltpu.VMEM((length, PAIR), BF),
                pltpu.VMEM((length, PAIR), BF),
                pltpu.VMEM((PAIR, length), BF),
                pltpu.VMEM((length, PAIR), F32),
                pltpu.VMEM((length, PAIR), F32),
            ],
        ),
        cost_estimate=pl.CostEstimate(
            flops=10 * length * length * wide,
            transcendentals=length * length * wide // PAIR,
            bytes_accessed=16 * length * wide,
        ),
        name="attend_back",
    )(pos, keep, queries, keys, values, grad_out, lse)


def piece_sizes(total, parts):
    granules = total // 8
    return [8 * (granules // parts + (1 if i < granules % parts else 0)) for i in range(parts)]


def to_slots(rows, parts):
    sizes = piece_sizes(rows.shape[0], parts)
    slot = max(sizes)
    out = []
    first = 0
    for size in sizes:
        piece = rows[first : first + size]
        if size < slot:
            piece = jnp.concatenate([piece, jnp.zeros((slot - size,) + rows.shape[1:], rows.dtype)])
        out.append(piece)
        first += size
    return jnp.stack(out)


def from_slots(slots, total):
    sizes = piece_sizes(total, slots.shape[-3])
    return jnp.concatenate(
        [slots[..., i, :size, :] for i, size in enumerate(sizes)], axis=-2
    )


def swap_core(value):
    count = lax.axis_size("seq")
    return lax.ppermute(value, "seq", [(i, i ^ 1) for i in range(count)])


def swap_y(value):
    count = lax.axis_size("seq")
    return lax.ppermute(value, "seq", [(i, i ^ 2) for i in range(count)])


def gather_four(value):
    near = swap_core(value)
    far = swap_y(value)
    return jnp.concatenate([value, near, far, swap_core(far)], axis=0)


def reduce_two(part):
    half = part.shape[0] // 2
    return part[:half] + swap_core(part[half:].astype(BF)).astype(F32)


def reduce_four(part):
    n = part.shape[0] // 4
    send = jnp.concatenate([part[n : 2 * n], part[3 * n :]], axis=0).astype(BF)
    kept = jnp.concatenate([part[:n], part[2 * n : 3 * n]], axis=0)
    both = kept + swap_core(send).astype(F32)
    return both[:n] + swap_y(both[n:].astype(BF)).astype(F32)


def local_fast(
    tokens,
    span_order,
    qkv_weight,
    out_weight,
    fc_weight,
    proj_weight,
    ln1_gain,
    ln1_bias,
    qv_bias,
    out_bias,
    ln2_gain,
    ln2_bias,
    fc_bias,
    proj_bias,
    out_grad,
):
    seqs = lax.axis_size("seq")
    dps = lax.axis_size("dp")
    rank = lax.axis_index("seq")
    y = rank // 2
    core = rank % 2
    local_len = tokens.shape[1]
    width = tokens.shape[2]
    full_len = local_len * seqs
    count = span_order.shape[1]
    heads = width // HEAD
    core_heads = (heads + 1) // 2
    slots = core_heads + core_heads % 2
    wide = slots * HEAD
    skip = (heads - core_heads) * HEAD
    hid = fc_weight.shape[1] // seqs
    pcols = proj_weight.shape[1]
    blocks = proj_weight.shape[0] // (seqs * hid)

    def pick(zero, one):
        return jnp.where(core == 0, zero, one)

    qkv_slots = to_slots(qkv_weight.T, seqs)
    out_slots = to_slots(out_weight.T, seqs)
    qs = qkv_slots.shape[1]
    os = out_slots.shape[1]
    first = lax.all_to_all(
        jnp.concatenate([qkv_slots, out_slots], axis=1), "seq", 0, 0
    )
    first = first.transpose(1, 0, 2).reshape(qs + os, width)
    first_all = lax.all_gather(first, ("dp", "seq"), axis=0).reshape(dps, seqs, qs + os, width)
    qkv_t = from_slots(first_all[:, :, :qs], qkv_weight.shape[1]).reshape(3, width, width)
    out_t = from_slots(first_all[:, :, qs:], out_weight.shape[1]).reshape(width, width)

    fc_pieces = fc_weight.T.reshape(seqs, hid, fc_weight.shape[0])
    proj_pieces = (
        proj_weight.T.reshape(pcols, blocks, seqs, hid)
        .transpose(2, 0, 1, 3)
        .reshape(seqs, pcols, blocks * hid)
    )
    second = lax.all_to_all(jnp.concatenate([fc_pieces, proj_pieces], axis=1), "seq", 0, 0)
    second = second.transpose(1, 0, 2).reshape(hid + pcols, width)
    fc_t = lax.all_gather(second[:hid], "dp", axis=0, tiled=True)
    proj_t = lax.all_gather(second[hid:], "dp", axis=0, tiled=True)

    vectors = jnp.concatenate(
        [ln1_gain, ln1_bias, qv_bias[0], qv_bias[1], out_bias, ln2_gain, ln2_bias, proj_bias, fc_bias]
    )
    vectors = lax.all_gather(vectors, "seq", axis=0)
    piece = ln1_gain.shape[0]
    gain_one, shift_one, q_shift, v_shift, out_shift, gain_two, shift_two, proj_shift = [
        vectors[:, i * piece : (i + 1) * piece].reshape(-1).astype(F32) for i in range(8)
    ]
    fc_all = vectors[:, 8 * piece :].reshape(dps, seqs, hid)
    fc_shift = lax.dynamic_index_in_dim(fc_all, rank, 1, False).reshape(-1).astype(F32)

    def own_rows(value):
        mine = lax.dynamic_index_in_dim(value, y, 0, False)
        other = lax.dynamic_index_in_dim(value, 1 - y, 0, False)
        return jnp.concatenate([mine, swap_y(other)], axis=0)

    def native_rows(value):
        mine, other = value[:local_len], swap_y(value[local_len:])
        return jnp.where(y == 0, jnp.stack([mine, other]), jnp.stack([other, mine]))

    tok = own_rows(tokens).astype(F32)
    grad_rows = own_rows(out_grad)
    grad_all = gather_four(grad_rows)
    ranks = jnp.stack([2 * y + core, 2 * (1 - y) + core, 2 * y + 1 - core, 2 * (1 - y) + 1 - core])
    per = count // seqs
    storage = (ranks[:, None] * per + jnp.arange(per, dtype=jnp.int32)[None]).reshape(-1)
    own_order = lax.dynamic_index_in_dim(span_order, y, 0, False)
    ids = jnp.arange(count, dtype=jnp.int32)
    held = jnp.sum(jnp.where(storage[:, None] == ids[None], own_order[None], 0), axis=1)
    pos = jnp.sum(jnp.where(held[None] == ids[:, None], ids[None], 0), axis=1).astype(jnp.int32)
    slot_ids = jnp.arange(slots, dtype=jnp.int32)
    keep = jnp.where(core == 0, slot_ids < core_heads, (slot_ids < core_heads) & (slot_ids >= 2 * core_heads - heads))
    keep = keep.astype(jnp.int32)

    normed_one = layer_norm(tok, gain_one, shift_one).astype(BF)
    normed_one = jnp.concatenate([normed_one, swap_core(normed_one)], axis=0)
    pad = jnp.zeros((skip + wide - width, width), BF)
    w_heads = []
    for i in range(3):
        rows = jnp.concatenate([qkv_t[i], pad], axis=0)
        w_heads.append(pick(rows[:wide], rows[skip : skip + wide]))
    w_core = jnp.concatenate(w_heads, axis=0)

    def core_vector(value):
        value = jnp.concatenate([value, jnp.zeros((skip + wide - width,), F32)])
        return pick(value[:wide], value[skip : skip + wide])

    b_core = jnp.concatenate([core_vector(q_shift), jnp.zeros((wide,), F32), core_vector(v_shift)])
    packed = (nt(normed_one, w_core) + b_core).astype(BF)
    queries, keys, values = packed[:, :wide], packed[:, wide : 2 * wide], packed[:, 2 * wide :]
    attended, lse = attend_fast(pos, keep, queries, keys, values)
    out_pad = jnp.concatenate([out_t, pad.T], axis=1)
    out_core = pick(out_pad[:, :wide], out_pad[:, skip : skip + wide])
    middle = tok + (reduce_two(nt(attended, out_core)) + out_shift)
    normed_two = layer_norm(middle, gain_two, shift_two).astype(BF)

    normed_all = gather_four(normed_two)
    hidden_pre = nt(normed_all, fc_t) + fc_shift
    hidden = smooth_gate(hidden_pre).astype(BF)
    grad_hidden = nt(grad_all, proj_t.T)
    grad_pre = gate_grad(hidden_pre, grad_hidden).astype(BF)
    grad_normed_two = reduce_four(nn(grad_pre, fc_t))
    proj_grad = tn(grad_all, hidden)
    fc_grad = tn(grad_pre, normed_all)
    result = middle + (reduce_four(nt(hidden, proj_t)) + proj_shift)
    output = native_rows(result.astype(BF))
    proj_part = lax.psum_scatter(proj_grad.astype(BF), "dp", scatter_dimension=0, tiled=True)
    fc_part = lax.psum_scatter(fc_grad.astype(BF), "dp", scatter_dimension=0, tiled=True)

    grad_mid_norm, grad_gain_two, grad_shift_two = norm_grad(
        middle, gain_two, shift_two, grad_normed_two
    )
    grad_middle = grad_rows.astype(F32) + grad_mid_norm
    grad_branch = grad_middle.astype(BF)
    branch_all = jnp.concatenate([grad_branch, swap_core(grad_branch)], axis=0)
    grad_attended = nn(branch_all, out_core).astype(BF)
    out_grad_core = tn(branch_all, attended)
    grad_q, grad_k, grad_v = attend_back_fast(
        pos, keep, queries, keys, values, grad_attended, lse
    )
    grad_packed = jnp.concatenate([grad_q, grad_k, grad_v], axis=1)
    qkv_grad_core = tn(grad_packed, normed_one).astype(BF)
    grad_normed_one = reduce_two(nn(grad_packed, w_core))
    grad_in_norm, grad_gain_one, grad_shift_one = norm_grad(
        tok, gain_one, shift_one, grad_normed_one
    )
    input_grad = native_rows((grad_middle + grad_in_norm).astype(BF))

    valid = core_heads * HEAD
    low = 2 * valid - width

    def both_cores(mine, other, axis):
        def cut(value, a, b):
            return lax.slice_in_dim(value, a, b, axis=axis)

        return pick(
            jnp.concatenate([cut(mine, 0, valid), cut(other, low, valid)], axis=axis),
            jnp.concatenate([cut(other, 0, valid), cut(mine, low, valid)], axis=axis),
        )

    other_qkv = swap_core(qkv_grad_core)
    qkv_full = jnp.concatenate(
        [
            both_cores(
                qkv_grad_core[i * wide : (i + 1) * wide], other_qkv[i * wide : (i + 1) * wide], 0
            )
            for i in range(3)
        ],
        axis=0,
    )
    out_low = out_grad_core.astype(BF)
    out_full = both_cores(out_low, swap_core(out_low), 1)
    send = jnp.concatenate(
        [
            jax.vmap(lambda rows: to_slots(rows, seqs))(qkv_full.reshape(dps, -1, width)),
            jax.vmap(lambda rows: to_slots(rows, seqs))(out_full.reshape(dps, -1, width)),
        ],
        axis=2,
    )
    keep_core = jnp.arange(seqs, dtype=jnp.int32) % 2 == core
    send = jnp.where(keep_core[None, :, None, None], send, jnp.zeros_like(send))
    first_part = lax.psum_scatter(
        send.reshape(dps * seqs * (qs + os), width), ("dp", "seq"), scatter_dimension=0, tiled=True
    )

    def spread(value):
        rows = value.shape[0]
        return lax.all_to_all(value.reshape(rows, seqs, -1).transpose(1, 0, 2), "seq", 0, 0)

    first_back = spread(first_part)
    qkv_weight_grad = from_slots(first_back[:, :qs], qkv_weight.shape[1]).T.astype(F32)
    out_weight_grad = from_slots(first_back[:, qs:], out_weight.shape[1]).T.astype(F32)
    fc_back = spread(fc_part)
    fc_weight_grad = fc_back.reshape(seqs * hid, -1).T.astype(F32)
    proj_back = spread(proj_part).reshape(seqs, pcols, blocks, hid)
    proj_weight_grad = proj_back.transpose(2, 0, 3, 1).reshape(-1, pcols).astype(F32)

    gq = jnp.sum(grad_q, axis=0, dtype=F32)[:valid]
    gv = jnp.sum(grad_v, axis=0, dtype=F32)[:valid]

    def whole(value):
        return pick(
            jnp.concatenate([value, jnp.zeros((width - valid,), F32)]),
            jnp.concatenate([jnp.zeros((width - valid,), F32), value]),
        )

    gf = jnp.sum(grad_pre, axis=0, dtype=F32).reshape(dps, 1, hid)
    gf = jnp.where(jnp.arange(seqs, dtype=jnp.int32)[None, :, None] == rank, gf, 0.0)
    rows = [
        grad_gain_one,
        grad_shift_one,
        whole(gq),
        whole(gv),
        jnp.sum(grad_branch, axis=0, dtype=F32),
        grad_gain_two,
        grad_shift_two,
        jnp.sum(grad_rows, axis=0, dtype=F32),
    ]
    summed = lax.psum(jnp.concatenate(rows + [gf.reshape(-1)]), ("dp", "seq"))
    mats = summed[: 8 * width].reshape(8, seqs, piece)
    mine = lax.dynamic_index_in_dim(mats, rank, 1, False)
    fc_vec = lax.dynamic_index_in_dim(summed[8 * width :].reshape(seqs, -1), rank, 0, False)
    return (
        output,
        input_grad,
        qkv_weight_grad,
        out_weight_grad,
        fc_weight_grad,
        proj_weight_grad,
        mine[0],
        mine[1],
        mine[2:4],
        mine[4],
        mine[5],
        mine[6],
        fc_vec,
        mine[7],
    )


def solution(mesh):
    placed = (
        P("dp", "seq", None),
        P("dp", None),
        P("seq", "dp"),
        P("seq", "dp"),
        P("seq", "dp"),
        P("seq", "dp"),
        P("seq"),
        P("seq"),
        P(None, "seq"),
        P("seq"),
        P("seq"),
        P("seq"),
        P("seq"),
        P("seq"),
        P("dp", "seq", None),
    )
    fast = mesh.shape["seq"] == 4
    return jax.shard_map(
        local_fast if fast else local,
        mesh=mesh,
        in_specs=placed,
        out_specs=(
            P("dp", "seq", None),
            P("dp", "seq", None),
            P("seq", "dp"),
            P("seq", "dp"),
            P("seq", "dp"),
            P("seq", "dp"),
            P("seq"),
            P("seq"),
            P(None, "seq"),
            P("seq"),
            P("seq"),
            P("seq"),
            P("seq"),
            P("seq"),
        ),
        check_vma=False,
    )
```
